256 devices in a mesh: section: 8 (over x, y_hi), dp: 32 (over y_lo, z, core).
Axes of the slice: x: 4, y: 4 (y_hi: 2, y_lo: 2; y = y_hi * 2 + y_lo), z: 8, core: 2. Of those that a mesh axis runs over, the one named last changes fastest.
Arguments:
- latent: bfloat16 [8192, 1536], P('dp'), may hold values from -6 to 6
- target: bfloat16 [8192, 1536], P('dp'), may hold values from -6 to 6
- camera_of_token: int32 [8192], P('dp'), may hold values from 0 to 5
- timestep_indices: int32 [2], replicated, may hold values from 0 to 49
- camera_embedding_table: bfloat16 [6, 1536], replicated, may hold values from -3 to 3
- timestep_embedding_table: bfloat16 [50, 1536], replicated, may hold values from -2.5 to 2.5
- layer_norm_gain: float32 [8, 1536], P('section'), may hold values from 0.25 to 1.75
- frozen_weight: bfloat16 [8, 1536, 1536], P('section', 'dp'), may hold values from -0.15625 to 0.15625
- adapter_down_weight: bfloat16 [8, 64, 1536], P('section'), may hold values from -0.15625 to 0.15625
- adapter_up_weight: bfloat16 [8, 64, 1536], P('section'), may hold values from -0.75 to 0.75
Outputs:
- grad_down: float32 [8, 64, 1536], P('section', None, 'dp')
- grad_up: float32 [8, 64, 1536], P('section', None, 'dp')
The draws below stay inside these ranges and needn't reach their ends.
Inputs may be any that keep to these rules, and one draw needn't show every extreme that they name: `timestep_indices`: indices of rows of timestep_embedding_table.
All inputs are finite; a program needn't handle non-finite values.
Results may differ from the reference program's by a relative error of at most 0.024.
Values may be sent and summed in bfloat16 or wider, within the bound.
No kernel may reach another device: no remote copies, remote signals or barrier semaphores. Data moves between devices by JAX's collectives and lax.ppermute only.
A program may use at most 64 MiB of HBM per device.

```python
import math
import jax
import jax.numpy as jnp
from jax import lax

HIDDEN_WIDTH = 1536
ADAPTER_RANK = 64
TOK_DEV = 256
VIEWS = 6
TSTEPS = 50
LAYER_COUNT = 8
TOKENS = 8192
N_DP = 32


def set_ends(values, stream_key, low, top_value):
    index_at = [jax.random.randint(jax.random.fold_in(stream_key, axis), (), 0, length) for axis, length in enumerate(values.shape)]
    longest = values.shape.index(max(values.shape))
    beside = index_at[:longest] + [(index_at[longest] + 1) % values.shape[longest]] + index_at[longest + 1:]
    return values.at[tuple(index_at)].set(low).at[tuple(beside)].set(top_value)


def with_spikes(drawn, own_key, source, target, shards_of, factor):
    owner, partner = [(jnp.arange(drawn.shape[axis_at]) // (drawn.shape[axis_at] // shards_of)).reshape([-1 if axis == axis_at else 1 for axis in range(drawn.ndim)]) for axis_at in (source, target)]
    chosen = jax.random.permutation(own_key, shards_of)[partner]
    strong = (owner == chosen) | (owner == (partner + shards_of // 2) % shards_of)
    return jnp.where(strong, factor * drawn, drawn)


def shard_levels(rng, extent, shards, smallest, largest):
    def one(position, parts):
        heights = jax.random.uniform(jax.random.fold_in(jax.random.fold_in(rng, 6), position), (parts,), jnp.float32, smallest / len(shards), largest / len(shards))
        return jnp.repeat(jnp.exp(heights), extent[position] // parts).reshape((-1,) + (1,) * (len(extent) - position - 1))

    factor_of = one(*shards[0])
    for cut in shards[1:]:
        factor_of = factor_of * one(*cut)
    return factor_of


def gaussian(own_key, dims, width, bound, cuts=(), kind=jnp.bfloat16):
    factor_of = shard_levels(own_key, dims, cuts, -0.22, 0.18) if cuts else 1.0
    values = jax.random.normal(own_key, dims, jnp.float32) * width * factor_of
    return jnp.minimum(jnp.maximum(values, -bound), bound).astype(kind)


def gaussian_with(rng, dims, scale, bound, shards, heavy, held_as=jnp.bfloat16):
    drawn = scale * jax.random.normal(rng, dims, jnp.float32)
    if shards:
        drawn = drawn * shard_levels(rng, dims, shards, -0.22, 0.18)
    return jnp.clip(with_spikes(drawn, jax.random.fold_in(rng, 3), *heavy), -bound, bound).astype(held_as)


def setup_inputs(seed: int = 0) -> dict:
    keys = jax.random.split(jax.random.key(seed), 11)
    return {
        "latent": gaussian(keys[0], (TOKENS, HIDDEN_WIDTH), 1.0, 6.0, ((0, 32),)),
        "target": gaussian_with(keys[1], (TOKENS, HIDDEN_WIDTH), 1.0, 6.0, ((0, 32),), (0, 1, 32, 2.75)),
        "camera_of_token": set_ends(jax.random.randint(keys[2], (TOKENS,), 0, VIEWS), jax.random.fold_in(keys[2], 1), 0, VIEWS - 1).astype(jnp.int32),
        "timestep_indices": jax.random.randint(keys[3], (2,), 0, TSTEPS).astype(jnp.int32),
        "camera_embedding_table": gaussian(keys[4], (VIEWS, HIDDEN_WIDTH), 0.5, 3.0),
        "timestep_embedding_table": gaussian(keys[5], (TSTEPS, HIDDEN_WIDTH), 0.3, 2.5),
        "layer_norm_gain": jnp.clip(1.0 + 0.15 * jax.random.normal(keys[6], (LAYER_COUNT, HIDDEN_WIDTH), jnp.float32), 0.25, 1.75),
        "frozen_weight": gaussian(keys[7], (LAYER_COUNT, HIDDEN_WIDTH, HIDDEN_WIDTH), HIDDEN_WIDTH ** -0.5, 0.15625, ((0, 8), (1, 32))),
        "adapter_down_weight": gaussian(keys[8], (LAYER_COUNT, ADAPTER_RANK, HIDDEN_WIDTH), HIDDEN_WIDTH ** -0.5, 0.15625, ((0, 8),)),
        "adapter_up_weight": gaussian(keys[9], (LAYER_COUNT, ADAPTER_RANK, HIDDEN_WIDTH), ADAPTER_RANK ** -0.5, 0.75, ((0, 8),)),
    }


BLEND = 0.5
ADAPTER_SCALE = 0.5
EPSILON = 1e-06

def forward_layer_pass(hidden_state, layer_weight, down_weight_rows, up_weight_rows, gain_row, modulate_row):
    hidden_float = hidden_state.astype(jnp.float32)
    inverse_rms = lax.rsqrt(lax.optimization_barrier(jnp.mean(hidden_float * hidden_float, axis=-1, keepdims=True)) + EPSILON)
    normalized_hidden = (hidden_float * inverse_rms * (gain_row * modulate_row)).astype(jnp.bfloat16)
    low_rank_hidden = lax.dot_general(normalized_hidden, down_weight_rows, (((1,), (1,)), ((), ())), preferred_element_type=jnp.float32).astype(jnp.bfloat16)
    preactivation = jnp.dot(normalized_hidden, layer_weight, preferred_element_type=jnp.float32) + ADAPTER_SCALE * jnp.dot(low_rank_hidden, up_weight_rows, preferred_element_type=jnp.float32)
    output = (hidden_float + jax.nn.silu(preactivation)).astype(jnp.bfloat16)
    return (output, normalized_hidden, low_rank_hidden, preactivation)

def backward_layer_pass(hidden_state, normalized_hidden, low_rank_hidden, preactivation, output_gradient, layer_weight, down_weight_rows, up_weight_rows, gain_row, modulate_row):
    sigmoid_value = jax.nn.sigmoid(preactivation)
    preactivation_gradient = (output_gradient * sigmoid_value * (1.0 + preactivation * (1.0 - sigmoid_value))).astype(jnp.bfloat16)
    low_rank_gradient = (ADAPTER_SCALE * lax.dot_general(preactivation_gradient, up_weight_rows, (((1,), (1,)), ((), ())), preferred_element_type=jnp.float32)).astype(jnp.bfloat16)
    norm_grad = lax.dot_general(preactivation_gradient, layer_weight, (((1,), (1,)), ((), ())), preferred_element_type=jnp.float32) + jnp.dot(low_rank_gradient, down_weight_rows, preferred_element_type=jnp.float32)
    up_gradient_term = ADAPTER_SCALE * lax.dot_general(low_rank_hidden, preactivation_gradient, (((0,), (0,)), ((), ())), preferred_element_type=jnp.float32)
    down_gradient_term = lax.dot_general(low_rank_gradient, normalized_hidden, (((0,), (0,)), ((), ())), preferred_element_type=jnp.float32)
    hidden_float = hidden_state.astype(jnp.float32)
    inverse_rms = lax.rsqrt(lax.optimization_barrier(jnp.mean(hidden_float * hidden_float, axis=-1, keepdims=True)) + EPSILON)
    scaled = hidden_float * inverse_rms
    scaled_grad = norm_grad * (gain_row * modulate_row)
    hidden_gradient = output_gradient + inverse_rms * (scaled_grad - scaled * lax.optimization_barrier(jnp.mean(scaled_grad * scaled, axis=-1, keepdims=True)))
    return (hidden_gradient, down_gradient_term, up_gradient_term)

def reference(latent, target, camera_of_token, timestep_indices, camera_embedding_table, timestep_embedding_table, layer_norm_gain, frozen_weight, adapter_down_weight, adapter_up_weight):
    timestep_modulation = 1.0 + jnp.dot(jax.nn.one_hot(timestep_indices, TSTEPS, dtype=jnp.bfloat16), timestep_embedding_table, preferred_element_type=jnp.float32)
    scale_factor = 1.0 / math.sqrt(TOKENS)

    def block_grads(totals, pieces):
        latent_rows, target_rows, camera_index = pieces
        camera_rows = jnp.dot(jax.nn.one_hot(camera_index, VIEWS, dtype=jnp.bfloat16), camera_embedding_table, preferred_element_type=jnp.float32)
        latent_now = latent_rows
        saved = []
        final_latent = latent_rows.astype(jnp.float32)
        for current_step in range(2):
            hidden_state = (latent_now.astype(jnp.float32) + camera_rows).astype(jnp.bfloat16)
            layer_inputs = []
            for current_layer in range(LAYER_COUNT):
                layer_inputs.append(hidden_state)
                hidden_state = forward_layer_pass(hidden_state, frozen_weight[current_layer], adapter_down_weight[current_layer], adapter_up_weight[current_layer], layer_norm_gain[current_layer], timestep_modulation[current_step])[0]
            saved.append(layer_inputs)
            blended = BLEND * (latent_now.astype(jnp.float32) + hidden_state.astype(jnp.float32))
            if current_step == 0:
                latent_now = blended.astype(jnp.bfloat16)
            else:
                final_latent = blended
        squashed = jnp.tanh(final_latent)
        adjoint = target_rows.astype(jnp.float32) * (1.0 - squashed * squashed) * scale_factor
        down_totals, up_totals = totals
        carried = jnp.zeros_like(adjoint)
        for current_step in (1, 0):
            if current_step == 1:
                output_gradient = BLEND * adjoint
            else:
                output_gradient = BLEND * (BLEND * adjoint + carried)
            for current_layer in reversed(range(LAYER_COUNT)):
                hidden_state = saved[current_step][current_layer]
                forward_pieces_saved = forward_layer_pass(hidden_state, frozen_weight[current_layer], adapter_down_weight[current_layer], adapter_up_weight[current_layer], layer_norm_gain[current_layer], timestep_modulation[current_step])
                hidden_gradient, down_gradient_term, up_gradient_term = backward_layer_pass(hidden_state, forward_pieces_saved[1], forward_pieces_saved[2], forward_pieces_saved[3], output_gradient, frozen_weight[current_layer], adapter_down_weight[current_layer], adapter_up_weight[current_layer], layer_norm_gain[current_layer], timestep_modulation[current_step])
                down_totals = down_totals.at[current_layer].add(down_gradient_term)
                up_totals = up_totals.at[current_layer].add(up_gradient_term)
                rounded = lax.optimization_barrier(hidden_gradient.astype(jnp.bfloat16))
                output_gradient = rounded.astype(jnp.float32)
            carried = output_gradient
        return ((down_totals, up_totals), jnp.zeros((), jnp.float32))
    zeros = jnp.zeros((LAYER_COUNT, ADAPTER_RANK, HIDDEN_WIDTH), jnp.float32)
    pieces = (latent.reshape(N_DP, TOK_DEV, HIDDEN_WIDTH), target.reshape(N_DP, TOK_DEV, HIDDEN_WIDTH), camera_of_token.reshape(N_DP, TOK_DEV))
    result = lax.scan(block_grads, (zeros, zeros), pieces)
    totals = result[0]
    return (totals[0], totals[1])
```

```python
import math

import jax
import jax.numpy as jnp
from jax import lax
from jax.experimental import pallas as pl
from jax.experimental.pallas import tpu as pltpu
from jax.sharding import PartitionSpec as P

BLEND = 0.5
ADAPTER_SCALE = 0.5
EPSILON = 1e-06
EXTRA = 8
F32 = jnp.float32
BF16 = jnp.bfloat16


def dot_nn(a, b):
    return lax.dot_general(a, b, (((1,), (0,)), ((), ())), preferred_element_type=F32)


def dot_nt(a, b):
    return lax.dot_general(a, b, (((1,), (1,)), ((), ())), preferred_element_type=F32)


def dot_tn(a, b):
    return lax.dot_general(a, b, (((0,), (0,)), ((), ())), preferred_element_type=F32)


def rows_kernel(
    layers,
    dp_size,
    part_rows,
    rank,
    scale_factor,
    latent_ref,
    target_ref,
    camera_ref,
    modulation_ref,
    pack_ref,
    grad_ref,
    weights,
    adapters,
    gains,
    hidden_store,
    normed_store,
    low_store,
    pre_store,
    grad_store,
    lowgrad_store,
    adjoint,
    sem,
):
    rows, width = latent_ref.shape
    adapter_blocks = 2 * rank // EXTRA

    def copies(layer):
        first = layer * dp_size
        return (
            pltpu.make_async_copy(
                pack_ref.at[pl.ds(first, dp_size), pl.ds(0, part_rows)],
                weights.at[layer],
                sem.at[0, layer],
            ),
            pltpu.make_async_copy(
                pack_ref.at[pl.ds(first, adapter_blocks), pl.ds(part_rows, EXTRA)],
                adapters.at[layer],
                sem.at[1, layer],
            ),
            pltpu.make_async_copy(
                pack_ref.at[pl.ds(first + adapter_blocks, 1), pl.ds(part_rows, EXTRA)],
                gains.at[layer],
                sem.at[2, layer],
            ),
        )

    for layer in range(layers):
        for one in copies(layer):
            one.start()

    def weight(layer):
        return weights[layer].reshape(width, width)

    def adapter(layer):
        both = adapters[layer].reshape(2 * rank, width)
        return both[:rank], both[rank:]

    def scale_row(layer, step):
        parts = gains[layer, 0].astype(F32)
        gain = (parts[0:1] + parts[1:2]) + parts[2:3]
        return gain * modulation_ref[pl.ds(step, 1), :]

    def forward(step, layer, hidden):
        slot = step * layers + layer
        hidden_store[slot] = hidden
        down, up = adapter(layer)
        hf = hidden.astype(F32)
        inverse = lax.rsqrt(jnp.mean(hf * hf, axis=-1, keepdims=True) + EPSILON)
        normed = (hf * inverse * scale_row(layer, step)).astype(BF16)
        low = dot_nt(normed, down).astype(BF16)
        pre = dot_nn(normed, weight(layer)) + ADAPTER_SCALE * dot_nn(low, up)
        normed_store[slot] = normed
        low_store[slot] = low
        pre_store[slot] = pre
        return (hf + pre * jax.nn.sigmoid(pre)).astype(BF16)

    def first_pass(layer, hidden):
        for one in copies(layer):
            one.wait()
        return forward(0, layer, hidden)

    latent = latent_ref[...].astype(F32)
    camera = camera_ref[...]
    hidden = lax.fori_loop(0, layers, first_pass, (latent + camera).astype(BF16))
    middle = (BLEND * (latent + hidden.astype(F32))).astype(BF16).astype(F32)
    hidden = lax.fori_loop(
        0, layers, lambda layer, h: forward(1, layer, h), (middle + camera).astype(BF16)
    )
    squashed = jnp.tanh(BLEND * (middle + hidden.astype(F32)))
    adjoint[...] = target_ref[...].astype(F32) * (1.0 - squashed * squashed) * scale_factor

    def backward(step, layer, cotangent):
        slot = step * layers + layer
        down, up = adapter(layer)
        pre = pre_store[slot]
        s = jax.nn.sigmoid(pre)
        pre_grad = (cotangent * s * (1.0 + pre * (1.0 - s))).astype(BF16)
        low_grad = (ADAPTER_SCALE * dot_nt(pre_grad, up)).astype(BF16)
        norm_grad = dot_nt(pre_grad, weight(layer)) + dot_nn(low_grad, down)
        hf = hidden_store[slot].astype(F32)
        inverse = lax.rsqrt(jnp.mean(hf * hf, axis=-1, keepdims=True) + EPSILON)
        y = hf * inverse
        g = norm_grad * scale_row(layer, step)
        result = cotangent + inverse * (g - y * jnp.mean(g * y, axis=-1, keepdims=True))
        return pre_grad, low_grad, result.astype(BF16).astype(F32)

    def last_step(i, cotangent):
        layer = layers - 1 - i
        pre_grad, low_grad, result = backward(1, layer, cotangent)
        grad_store[layer] = pre_grad
        lowgrad_store[layer] = low_grad
        return result

    def first_step(i, cotangent):
        layer = layers - 1 - i
        pre_grad, low_grad, result = backward(0, layer, cotangent)
        both = layers + layer
        pre_both = jnp.concatenate([pre_grad, grad_store[layer]], axis=0)
        lg_both = jnp.concatenate([low_grad, lowgrad_store[layer]], axis=0)
        low_both = jnp.concatenate([low_store[layer], low_store[both]], axis=0)
        normed_both = jnp.concatenate([normed_store[layer], normed_store[both]], axis=0)
        grad_ref[layer, :, 0:rank] = dot_tn(normed_both, lg_both).astype(grad_ref.dtype)
        grad_ref[layer, :, rank:] = (ADAPTER_SCALE * dot_tn(pre_both, low_both)).astype(grad_ref.dtype)
        return result

    entering = lax.fori_loop(0, layers, last_step, BLEND * adjoint[...])
    lax.fori_loop(0, layers, first_step, BLEND * (BLEND * adjoint[...] + entering))


def row_gradients(latent, target, camera, modulation, pack, layers, dp_size, rank, scale_factor, dtype):
    rows, width = latent.shape
    part_rows = width // dp_size
    vmem = pl.BlockSpec(memory_space=pltpu.VMEM)

    def body(*refs):
        rows_kernel(layers, dp_size, part_rows, rank, scale_factor, *refs)

    return pl.pallas_call(
        body,
        out_shape=jax.ShapeDtypeStruct((layers, width, 2 * rank), dtype),
        in_specs=[vmem, vmem, vmem, vmem, pl.BlockSpec(memory_space=pl.ANY)],
        out_specs=vmem,
        scratch_shapes=[
            pltpu.VMEM((layers, dp_size, part_rows, width), BF16),
            pltpu.VMEM((layers, 2 * rank // EXTRA, EXTRA, width), BF16),
            pltpu.VMEM((layers, 1, EXTRA, width), BF16),
            pltpu.VMEM((2 * layers, rows, width), BF16),
            pltpu.VMEM((2 * layers, rows, width), BF16),
            pltpu.VMEM((2 * layers, rows, rank), BF16),
            pltpu.VMEM((2 * layers, rows, width), F32),
            pltpu.VMEM((layers, rows, width), BF16),
            pltpu.VMEM((layers, rows, rank), BF16),
            pltpu.VMEM((rows, width), F32),
            pltpu.SemaphoreType.DMA((3, layers)),
        ],
        compiler_params=pltpu.CompilerParams(vmem_limit_bytes=61 * 1024 * 1024),
        name="row_gradients",
    )(latent, target, camera, modulation, pack)


def exchange_and_add(parts, axis):
    count = lax.axis_size(axis)
    parts = parts.reshape(count, -1, parts.shape[-1])
    return lax.all_to_all(parts, axis, 0, 0, tiled=True).astype(F32).sum(0)


def local(
    latent,
    target,
    camera_of_token,
    timestep_indices,
    camera_embedding_table,
    timestep_embedding_table,
    layer_norm_gain,
    frozen_weight,
    adapter_down_weight,
    adapter_up_weight,
):
    sections = lax.axis_size("section")
    dp_size = lax.axis_size("dp")
    section = lax.axis_index("section")
    lane = lax.axis_index("dp")
    rank, width = adapter_down_weight.shape[1:]
    rows = latent.shape[0] // sections
    scale_factor = 1.0 / math.sqrt(latent.shape[0] * dp_size)
    adapter_rows = jnp.concatenate([adapter_down_weight[0], adapter_up_weight[0]], axis=0)
    adapter_blocks = 2 * rank // EXTRA
    mine = lax.dynamic_slice(
        adapter_rows, (EXTRA * jnp.minimum(lane, adapter_blocks - 1), 0), (EXTRA, width)
    )
    gain = layer_norm_gain
    high = lax.reduce_precision(gain, 8, 7)
    middle = lax.reduce_precision(gain - high, 8, 7)
    lowest = gain - high - middle
    gain_rows = jnp.concatenate(
        [high, middle, lowest, jnp.zeros((EXTRA - 3, width), F32)], axis=0
    ).astype(BF16)
    extra = jnp.where(lane < adapter_blocks, mine, gain_rows)
    own = jnp.concatenate([frozen_weight[0], extra], axis=0)
    pack = lax.all_gather(own, ("section", "dp"), axis=0, tiled=False)

    def my_rows(a):
        return lax.dynamic_slice_in_dim(a, section * rows, rows, 0)

    camera_rows = jnp.dot(
        jax.nn.one_hot(my_rows(camera_of_token), camera_embedding_table.shape[0], dtype=BF16),
        camera_embedding_table,
        preferred_element_type=F32,
    )
    modulation = 1.0 + jnp.dot(
        jax.nn.one_hot(timestep_indices, timestep_embedding_table.shape[0], dtype=BF16),
        timestep_embedding_table,
        preferred_element_type=F32,
    )
    grads = row_gradients(
        my_rows(latent),
        my_rows(target),
        camera_rows,
        modulation,
        pack,
        sections,
        dp_size,
        rank,
        scale_factor,
        BF16,
    )
    over_sections = exchange_and_add(grads, "section")
    summed = exchange_and_add(over_sections.astype(BF16), "dp")
    turned = summed.T
    return turned[None, :rank], turned[None, rank:]


def solution(mesh):
    in_specs = (
        P("dp", None),
        P("dp", None),
        P("dp"),
        P(),
        P(),
        P(),
        P("section", None),
        P("section", "dp", None),
        P("section", None, None),
        P("section", None, None),
    )
    out_specs = (P("section", None, "dp"), P("section", None, "dp"))
    return jax.shard_map(local, mesh=mesh, in_specs=in_specs, out_specs=out_specs, check_vma=False)
```

```python
import math

import jax
import jax.numpy as jnp
from jax import lax
from jax.experimental import pallas as pl
from jax.experimental.pallas import tpu as pltpu
from jax.sharding import PartitionSpec as P

BLEND = 0.5
ADAPTER_SCALE = 0.5
EPSILON = 1e-06
EXTRA = 8
EVERYWHERE = ("section", "dp")
SIZES = {"x": 4, "y": 4, "z": 8}
PART = 16
F32 = jnp.float32
BF16 = jnp.bfloat16


def dot_nn(a, b):
    return lax.dot_general(a, b, (((1,), (0,)), ((), ())), preferred_element_type=F32)


def dot_nt(a, b):
    return lax.dot_general(a, b, (((1,), (1,)), ((), ())), preferred_element_type=F32)


def dot_tn(a, b):
    return lax.dot_general(a, b, (((0,), (0,)), ((), ())), preferred_element_type=F32)


def ring_offsets(count):
    offsets = [0]
    for distance in range(1, count // 2 + 1):
        offsets.append(distance)
        if 2 * distance < count:
            offsets.append(-distance)
    return offsets


def rows_kernel(
    layers,
    rank,
    scale_factor,
    place_ref,
    latent_ref,
    target_ref,
    camera_ref,
    modulation_ref,
    *refs,
):
    piece_total = 2 * (SIZES["x"] + SIZES["y"])
    sides = refs[:2]
    last = refs[2]
    refs = refs[3:]
    pieces = refs[:piece_total]
    keep_ref, send_ref = refs[piece_total : piece_total + 2]
    run_rows(
        layers,
        rank,
        scale_factor,
        place_ref,
        latent_ref,
        target_ref,
        camera_ref,
        modulation_ref,
        sides,
        last,
        pieces,
        keep_ref,
        send_ref,
        *refs[piece_total + 2 :],
    )


def run_rows(
    layers,
    rank,
    scale_factor,
    place_ref,
    latent_ref,
    target_ref,
    camera_ref,
    modulation_ref,
    sides,
    last,
    pieces,
    keep_ref,
    send_ref,
    weights,
    side,
    hidden_store,
    normed_store,
    low_store,
    pre_store,
    grad_store,
    lowgrad_store,
    adjoint,
    sem,
    side_sem,
):
    rows, width = latent_ref.shape
    core = place_ref[3]

    copies = []
    number = 0
    for axis, name in enumerate(("x", "y")):
        count = SIZES[name]
        for half in range(2):
            owner = core if half == 0 else 1 - core
            sense = 1 - 2 * owner
            for offset in ring_offsets(count):
                at = lax.rem(place_ref[axis] - sense * offset + 2 * count, count)
                if name == "x":
                    home = weights.at[at, :, :, :, owner, pl.ds(0, PART)]
                else:
                    home = weights.at[:, at // 2, lax.rem(at, 2), :, owner, pl.ds(PART, PART)]
                copies.append(pltpu.make_async_copy(pieces[number], home, sem.at[number]))
                number += 1
    for z in range(SIZES["z"]):
        for owner in range(2):
            home = weights.at[:, :, :, z, owner, pl.ds(2 * PART, PART)]
            copies.append(pltpu.make_async_copy(last.at[2 * z + owner], home, sem.at[number]))
            number += 1
    for half in range(2):
        owner = core if half == 0 else 1 - core
        copies.append(pltpu.make_async_copy(sides[half], side.at[owner], side_sem.at[half]))
    for one in copies:
        one.start()
    for one in copies:
        one.wait()

    def weight(layer):
        return weights[layer // 2, lax.rem(layer, 2)].reshape(width, width)

    def adapter(layer):
        x, h = layer // 2, lax.rem(layer, 2)
        return side[0, x, h, 0:rank], side[1, x, h, 0:rank]

    def scale_row(layer, step):
        parts = side[0, layer // 2, lax.rem(layer, 2), rank:].astype(F32)
        gain = (parts[0:1] + parts[1:2]) + parts[2:3]
        return gain * modulation_ref[pl.ds(step, 1), :]

    def forward(step, layer, hidden):
        slot = step * layers + layer
        hidden_store[slot] = hidden
        down, up = adapter(layer)
        hf = hidden.astype(F32)
        inverse = lax.rsqrt(jnp.mean(hf * hf, axis=-1, keepdims=True) + EPSILON)
        normed = (hf * inverse * scale_row(layer, step)).astype(BF16)
        low = dot_nt(normed, down).astype(BF16)
        pre = dot_nn(normed, weight(layer)) + ADAPTER_SCALE * dot_nn(low, up)
        normed_store[slot] = normed
        low_store[slot] = low
        pre_store[slot] = pre
        return (hf + pre * jax.nn.sigmoid(pre)).astype(BF16)

    latent = latent_ref[...].astype(F32)
    camera = camera_ref[...]
    hidden = lax.fori_loop(
        0, layers, lambda layer, h: forward(0, layer, h), (latent + camera).astype(BF16)
    )
    middle = (BLEND * (latent + hidden.astype(F32))).astype(BF16).astype(F32)
    hidden = lax.fori_loop(
        0, layers, lambda layer, h: forward(1, layer, h), (middle + camera).astype(BF16)
    )
    squashed = jnp.tanh(BLEND * (middle + hidden.astype(F32)))
    adjoint[...] = target_ref[...].astype(F32) * (1.0 - squashed * squashed) * scale_factor

    def backward(step, layer, cotangent):
        slot = step * layers + layer
        down, up = adapter(layer)
        pre = pre_store[slot]
        s = jax.nn.sigmoid(pre)
        pre_grad = (cotangent * s * (1.0 + pre * (1.0 - s))).astype(BF16)
        low_grad = (ADAPTER_SCALE * dot_nt(pre_grad, up)).astype(BF16)
        norm_grad = dot_nt(pre_grad, weight(layer)) + dot_nn(low_grad, down)
        hf = hidden_store[slot].astype(F32)
        inverse = lax.rsqrt(jnp.mean(hf * hf, axis=-1, keepdims=True) + EPSILON)
        y = hf * inverse
        g = norm_grad * scale_row(layer, step)
        result = cotangent + inverse * (g - y * jnp.mean(g * y, axis=-1, keepdims=True))
        return pre_grad, low_grad, result.astype(BF16).astype(F32)

    def last_step(i, cotangent):
        layer = layers - 1 - i
        pre_grad, low_grad, result = backward(1, layer, cotangent)
        grad_store[layer] = pre_grad
        lowgrad_store[layer] = low_grad
        return result

    def first_step(i, cotangent):
        layer = layers - 1 - i
        pre_grad, low_grad, result = backward(0, layer, cotangent)
        both = layers + layer
        pre_both = jnp.concatenate([pre_grad, grad_store[layer]], axis=0)
        lg_both = jnp.concatenate([low_grad, lowgrad_store[layer]], axis=0)
        low_both = jnp.concatenate([low_store[layer], low_store[both]], axis=0)
        normed_both = jnp.concatenate([normed_store[layer], normed_store[both]], axis=0)
        for first, term in (
            (0, dot_tn(normed_both, lg_both)),
            (rank, ADAPTER_SCALE * dot_tn(pre_both, low_both)),
        ):
            columns = term.reshape(-1, 2, keep_ref.shape[2], rank)
            here = core == 0
            keep_ref[layer, :, :, first : first + rank] = jnp.where(here, columns[:, 0], columns[:, 1])
            send_ref[layer, :, :, first : first + rank] = jnp.where(
                here, columns[:, 1], columns[:, 0]
            ).astype(BF16)
        return result

    entering = lax.fori_loop(0, layers, last_step, BLEND * adjoint[...])
    lax.fori_loop(0, layers, first_step, BLEND * (BLEND * adjoint[...] + entering))


def row_gradients(
    place, latent, target, camera, modulation, sides, last, pieces, layers, rank, chunk, scale_factor
):
    rows, width = latent.shape
    vmem = pl.BlockSpec(memory_space=pltpu.VMEM)
    hbm = pl.BlockSpec(memory_space=pltpu.HBM)
    half = (layers, width // (2 * chunk), chunk, 2 * rank)

    def body(*refs):
        rows_kernel(layers, rank, scale_factor, *refs)

    return pl.pallas_call(
        body,
        out_shape=(jax.ShapeDtypeStruct(half, F32), jax.ShapeDtypeStruct(half, BF16)),
        in_specs=[pl.BlockSpec(memory_space=pltpu.SMEM)] + [vmem] * 4 + [hbm] * (3 + len(pieces)),
        out_specs=(vmem, vmem),
        scratch_shapes=[
            pltpu.VMEM((4, 2, 2, 8, 2, 3 * PART, width), BF16),
            pltpu.VMEM((2,) + sides[0].shape, BF16),
            pltpu.VMEM((2 * layers, rows, width), BF16),
            pltpu.VMEM((2 * layers, rows, width), BF16),
            pltpu.VMEM((2 * layers, rows, rank), BF16),
            pltpu.VMEM((2 * layers, rows, width), F32),
            pltpu.VMEM((layers, rows, width), BF16),
            pltpu.VMEM((layers, rows, rank), BF16),
            pltpu.VMEM((rows, width), F32),
            pltpu.SemaphoreType.DMA((len(pieces) + last.shape[0],)),
            pltpu.SemaphoreType.DMA((2,)),
        ],
        compiler_params=pltpu.CompilerParams(vmem_limit_bytes=61 * 1024 * 1024),
        name="row_gradients",
    )(place, latent, target, camera, modulation, *sides, last, *pieces)


def device_number(x, y, z, core):
    return (x * 2 + y // 2) * 32 + (y % 2) * 16 + z * 2 + core


def route(axis, sign):
    pairs = []
    for x in range(SIZES["x"]):
        for y in range(SIZES["y"]):
            for z in range(SIZES["z"]):
                for core in range(2):
                    to = {"x": x, "y": y, "z": z}
                    step = sign if core == 0 else -sign
                    if axis == "half":
                        to["y"] = (y + 2) % SIZES["y"]
                    else:
                        to[axis] = (to[axis] + step) % SIZES[axis]
                    pairs.append((device_number(x, y, z, core), device_number(core=core, **to)))
    return pairs


def other_core(block):
    pairs = [(i, i ^ 1) for i in range(256)]
    return lax.ppermute(block, EVERYWHERE, pairs)


def together(*arrays):
    return lax.optimization_barrier(arrays)


def onwards(block, axis):
    return lax.ppermute(block, EVERYWHERE, route(axis, 1))


def back(block, axis):
    return lax.ppermute(block, EVERYWHERE, route(axis, -1))


def ring_blocks(block, axis):
    a = onwards(block, axis)
    return [block, a, back(block, axis), onwards(a, axis)]


def in_line(blocks, place, axis, before=0, split=1):
    count = len(blocks)
    rows = blocks[0].shape[-2] // split
    shape = blocks[0].shape[:-2] + (rows, blocks[0].shape[-1])
    shape = shape[:before] + (count,) + shape[before:]

    def body(place_ref, *refs):
        for i, offset in enumerate(ring_offsets(count)):
            if axis == "half":
                at = lax.rem(place_ref[1] // 2 + offset, 2)
            else:
                sense = 1 - 2 * place_ref[3]
                at = place_ref[list(SIZES).index(axis)] - sense * offset
                at = lax.rem(at + 2 * count, count)
            for half in range(split):
                block = refs[i][..., half * rows : (half + 1) * rows, :]
                out = refs[count + half]
                if before == 0:
                    out[at] = block
                else:
                    out[:, at] = block

    vmem = pl.BlockSpec(memory_space=pltpu.VMEM)
    out_shape = (jax.ShapeDtypeStruct(shape, blocks[0].dtype),) * split
    return pl.pallas_call(
        body,
        out_shape=out_shape,
        in_specs=[pl.BlockSpec(memory_space=pltpu.SMEM)] + [vmem] * count,
        out_specs=(vmem,) * split,
        compiler_params=pltpu.CompilerParams(vmem_limit_bytes=8 * 1024 * 1024),
        name="in_line_" + axis,
    )(place, *blocks)


def gathered_rows(rows, place):
    width = rows.shape[1]
    c, ab = rows[2 * PART :], rows[: 2 * PART]
    c1, c2, z1, y1 = onwards(c, "y"), back(c, "y"), onwards(ab, "z"), back(ab, "z")
    c1, c2, z1, y1 = together(c1, c2, z1, y1)
    c3, z2, y2 = together(onwards(c1, "y"), onwards(z1, "z"), back(y1, "z"))
    c = in_line([c, c1, c2, c3], place, "y")[0]
    c1, c2, z3, y3 = together(onwards(c, "x"), back(c, "x"), onwards(z2, "z"), back(y2, "z"))
    c3, z4 = together(onwards(c1, "x"), onwards(z3, "z"))
    c = in_line([c, c1, c2, c3], place, "x")[0]
    same_line = [[16 * low + i for i in range(16)] for low in range(2)]
    last = lax.all_gather(
        c.reshape(4, 2, 2, PART, width), "dp", axis=0, tiled=False, axis_index_groups=same_line
    )
    a, b = in_line([ab, z1, y1, z2, y2, z3, y3, z4], place, "z", split=2)
    a = in_line(ring_blocks(a, "y"), place, "y")[0].reshape(2, 2, 8, PART, width)
    b = in_line(ring_blocks(b, "x"), place, "x")[0]
    a1, b1 = onwards(a, "x"), onwards(b, "y")
    a2, b2 = back(a, "x"), back(b, "y")
    a, a1 = together(a, a1)
    b, b1 = together(b, b1)
    a3, b3 = onwards(a1, "x"), onwards(b1, "y")
    pieces = []
    for mine in ([a, a1, a2, a3], [b, b1, b2, b3]):
        pieces += mine + [other_core(piece) for piece in mine]
    return last, pieces


def gathered_sides(own, place):
    both = in_line([own, lax.ppermute(own, EVERYWHERE, route("half", 1))], place, "half")[0]
    mine = in_line(ring_blocks(both, "x"), place, "x")[0]
    return mine, other_core(mine)


def exchange_and_add(parts, axis, groups=None):
    received = lax.all_to_all(parts, axis, 0, 0, axis_index_groups=groups, tiled=True)
    return received.astype(F32).sum(0)


def local(
    latent,
    target,
    camera_of_token,
    timestep_indices,
    camera_embedding_table,
    timestep_embedding_table,
    layer_norm_gain,
    frozen_weight,
    adapter_down_weight,
    adapter_up_weight,
):
    sections = lax.axis_size("section")
    dp_size = lax.axis_size("dp")
    section = lax.axis_index("section")
    lane = lax.axis_index("dp")
    rank, width = adapter_down_weight.shape[1:]
    rows = latent.shape[0] // sections
    scale_factor = 1.0 / math.sqrt(latent.shape[0] * dp_size)
    place = jnp.stack(
        [section // 2, lax.rem(section, 2) * 2 + lane // 16, lax.rem(lane // 2, 8), lax.rem(lane, 2)]
    ).astype(jnp.int32)
    last, pieces = gathered_rows(frozen_weight[0], place)
    gain = layer_norm_gain
    high = lax.reduce_precision(gain, 8, 7)
    middle = lax.reduce_precision(gain - high, 8, 7)
    lowest = gain - high - middle
    gain_rows = jnp.concatenate([high, middle, lowest, jnp.zeros((EXTRA - 3, width), F32)], axis=0)
    adapter = jnp.where(place[3] == 0, adapter_down_weight[0], adapter_up_weight[0])
    sides = gathered_sides(jnp.concatenate([adapter, gain_rows.astype(BF16)], axis=0), place)

    def my_rows(a):
        return lax.dynamic_slice_in_dim(a, section * rows, rows, 0)

    camera_rows = jnp.dot(
        jax.nn.one_hot(my_rows(camera_of_token), camera_embedding_table.shape[0], dtype=BF16),
        camera_embedding_table,
        preferred_element_type=F32,
    )
    modulation = 1.0 + jnp.dot(
        jax.nn.one_hot(timestep_indices, timestep_embedding_table.shape[0], dtype=BF16),
        timestep_embedding_table,
        preferred_element_type=F32,
    )
    keep, send = row_gradients(
        place,
        my_rows(latent),
        my_rows(target),
        camera_rows,
        modulation,
        sides,
        last,
        pieces,
        sections,
        rank,
        width // dp_size,
        scale_factor,
    )
    on_chip = (keep + other_core(send).astype(F32)).astype(BF16)
    over_sections = exchange_and_add(on_chip, "section")
    same_core = [[i for i in range(32) if i % 2 == core] for core in range(2)]
    summed = exchange_and_add(over_sections.astype(BF16), "dp", same_core)
    turned = summed.T
    return turned[None, :rank], turned[None, rank:]


def solution(mesh):
    in_specs = (
        P("dp", None),
        P("dp", None),
        P("dp"),
        P(),
        P(),
        P(),
        P("section", None),
        P("section", "dp", None),
        P("section", None, None),
        P("section", None, None),
    )
    out_specs = (P("section", None, "dp"), P("section", None, "dp"))
    return jax.shard_map(local, mesh=mesh, in_specs=in_specs, out_specs=out_specs, check_vma=False)
```

```python
import math

import jax
import jax.numpy as jnp
from jax import lax
from jax.experimental import pallas as pl
from jax.experimental.pallas import tpu as pltpu
from jax.sharding import PartitionSpec as P

BLEND = 0.5
ADAPTER_SCALE = 0.5
EPSILON = 1e-06
EXTRA = 8
EVERYWHERE = ("section", "dp")
SIZES = {"x": 4, "y": 4, "z": 8}
PART = 16
CHUNK = 512
F32 = jnp.float32
BF16 = jnp.bfloat16


def dot_nn(a, b):
    return lax.dot_general(a, b, (((1,), (0,)), ((), ())), preferred_element_type=F32)


def dot_nt(a, b):
    return lax.dot_general(a, b, (((1,), (1,)), ((), ())), preferred_element_type=F32)


def dot_tn(a, b):
    return lax.dot_general(a, b, (((0,), (0,)), ((), ())), preferred_element_type=F32)


def ring_offsets(count):
    offsets = [0]
    for distance in range(1, count // 2 + 1):
        offsets.append(distance)
        if 2 * distance < count:
            offsets.append(-distance)
    return offsets


def rows_kernel(
    layers,
    rank,
    scale_factor,
    place_ref,
    latent_ref,
    target_ref,
    camera_ref,
    modulation_ref,
    *refs,
):
    piece_total = 2 * (SIZES["x"] + SIZES["y"])
    sides = refs[:2]
    last = refs[2]
    refs = refs[3:]
    pieces = refs[:piece_total]
    keep_ref, send_ref = refs[piece_total : piece_total + 2]
    run_rows(
        layers,
        rank,
        scale_factor,
        place_ref,
        latent_ref,
        target_ref,
        camera_ref,
        modulation_ref,
        sides,
        last,
        pieces,
        keep_ref,
        send_ref,
        *refs[piece_total + 2 :],
    )


def run_rows(
    layers,
    rank,
    scale_factor,
    place_ref,
    latent_ref,
    target_ref,
    camera_ref,
    modulation_ref,
    sides,
    last,
    pieces,
    keep_ref,
    send_ref,
    weights,
    side,
    hidden_store,
    normed_store,
    low_store,
    slope_store,
    grad_store,
    lowgrad_store,
    inverse_store,
    adjoint,
    sem,
    side_sem,
):
    rows, width = latent_ref.shape
    core = place_ref[3]

    for half in range(2):
        owner = core if half == 0 else 1 - core
        pltpu.make_async_copy(sides[half], side.at[owner], side_sem.at[half]).start()
    count = SIZES["x"]
    arrivals = [
        (half, i, core if half == 0 else 1 - core, offset)
        for half in range(2)
        for i, offset in enumerate(ring_offsets(count))
    ]

    def position(axis, owner, offset):
        return lax.rem(place_ref[axis] - (1 - 2 * owner) * offset + 2 * count, count)

    def fetch(x):
        for half, i, owner, offset in arrivals:
            home = weights.at[x, :, :, :, owner, pl.ds(0, PART)]
            one = pltpu.make_async_copy(pieces[count * half + i], home, sem.at[x])
            pl.when(position(0, owner, offset) == x)(one.start)
            at = position(1, owner, offset)
            home = weights.at[x, at // 2, lax.rem(at, 2), :, owner, pl.ds(PART, PART)]
            block = pieces[count * (2 + half) + i]
            pltpu.make_async_copy(block.at[x], home, sem.at[x]).start()
        for z in range(SIZES["z"]):
            for owner in range(2):
                home = weights.at[x, :, :, z, owner, pl.ds(2 * PART, PART)]
                pltpu.make_async_copy(last.at[2 * z + owner, x], home, sem.at[x]).start()

    fetch(0)

    def arrive(x):
        pltpu.make_async_copy(weights.at[x], weights.at[x], sem.at[x]).wait()

    def weight(layer):
        return weights[layer // 2, lax.rem(layer, 2)].reshape(width, width)

    def adapter(layer):
        x, h = layer // 2, lax.rem(layer, 2)
        return side[0, x, h, 0:rank], side[1, x, h, 0:rank]

    def scale_row(layer, step):
        parts = side[0, layer // 2, lax.rem(layer, 2), rank:].astype(F32)
        gain = (parts[0:1] + parts[1:2]) + parts[2:3]
        return gain * modulation_ref[pl.ds(step, 1), :]

    def forward(step, layer, hidden):
        slot = step * layers + layer
        hidden_store[slot] = hidden
        down, up = adapter(layer)
        hf = hidden.astype(F32)
        inverse = lax.rsqrt(jnp.mean(hf * hf, axis=-1, keepdims=True) + EPSILON)
        inverse_store[slot] = inverse
        normed = (hf * inverse * scale_row(layer, step)).astype(BF16)
        low = dot_nt(normed, down).astype(BF16)
        pre = dot_nn(normed, weight(layer)) + ADAPTER_SCALE * dot_nn(low, up)
        normed_store[slot] = normed
        low_store[slot] = low
        s = jax.nn.sigmoid(pre)
        slope_store[slot] = s * (1.0 + pre * (1.0 - s))
        return (hf + pre * s).astype(BF16)

    latent = latent_ref[...].astype(F32)
    camera = camera_ref[...]
    for half in range(2):
        owner = core if half == 0 else 1 - core
        pltpu.make_async_copy(sides[half], side.at[owner], side_sem.at[half]).wait()

    def first_pass(layer, h):
        x = layer // 2
        first = lax.rem(layer, 2) == 0
        pl.when(first)(lambda: arrive(x))
        pl.when(first & (x + 1 < count))(lambda: fetch(x + 1))
        return forward(0, layer, h)

    hidden = lax.fori_loop(0, layers, first_pass, (latent + camera).astype(BF16))
    middle = (BLEND * (latent + hidden.astype(F32))).astype(BF16).astype(F32)
    hidden = lax.fori_loop(
        0, layers, lambda layer, h: forward(1, layer, h), (middle + camera).astype(BF16)
    )
    squashed = jnp.tanh(BLEND * (middle + hidden.astype(F32)))
    adjoint[...] = target_ref[...].astype(F32) * (1.0 - squashed * squashed) * scale_factor

    def backward(step, layer, cotangent):
        slot = step * layers + layer
        down, up = adapter(layer)
        pre_grad = (cotangent * slope_store[slot]).astype(BF16)
        low_grad = (ADAPTER_SCALE * dot_nt(pre_grad, up)).astype(BF16)
        w = weight(layer)
        norm_grad = jnp.concatenate(
            [
                dot_nt(pre_grad, w[j : j + CHUNK]) + dot_nn(low_grad, down[:, j : j + CHUNK])
                for j in range(0, width, CHUNK)
            ],
            axis=1,
        )
        hf = hidden_store[slot].astype(F32)
        inverse = inverse_store[slot]
        y = hf * inverse
        g = norm_grad * scale_row(layer, step)
        result = cotangent + inverse * (g - y * jnp.mean(g * y, axis=-1, keepdims=True))
        return pre_grad, low_grad, result.astype(BF16).astype(F32)

    def last_step(i, cotangent):
        layer = layers - 1 - i
        pre_grad, low_grad, result = backward(1, layer, cotangent)
        grad_store[layer] = pre_grad
        lowgrad_store[layer] = low_grad
        return result

    def first_step(i, cotangent):
        layer = layers - 1 - i
        pre_grad, low_grad, result = backward(0, layer, cotangent)
        both = layers + layer
        pre_both = jnp.concatenate([pre_grad, grad_store[layer]], axis=0)
        lg_both = jnp.concatenate([low_grad, lowgrad_store[layer]], axis=0)
        low_both = jnp.concatenate([low_store[layer], low_store[both]], axis=0)
        normed_both = jnp.concatenate([normed_store[layer], normed_store[both]], axis=0)
        for first, term in (
            (0, dot_tn(normed_both, lg_both)),
            (rank, ADAPTER_SCALE * dot_tn(pre_both, low_both)),
        ):
            columns = term.reshape(-1, 2, keep_ref.shape[2], rank)
            here = core == 0
            keep_ref[layer, :, :, first : first + rank] = jnp.where(here, columns[:, 0], columns[:, 1])
            send_ref[layer, :, :, first : first + rank] = jnp.where(
                here, columns[:, 1], columns[:, 0]
            ).astype(BF16)
        return result

    entering = lax.fori_loop(0, layers, last_step, BLEND * adjoint[...])
    lax.fori_loop(0, layers, first_step, BLEND * (BLEND * adjoint[...] + entering))


def row_gradients(
    place, latent, target, camera, modulation, sides, last, pieces, layers, rank, chunk, scale_factor
):
    rows, width = latent.shape
    vmem = pl.BlockSpec(memory_space=pltpu.VMEM)
    hbm = pl.BlockSpec(memory_space=pltpu.HBM)
    half = (layers, width // (2 * chunk), chunk, 2 * rank)

    def body(*refs):
        rows_kernel(layers, rank, scale_factor, *refs)

    return pl.pallas_call(
        body,
        out_shape=(jax.ShapeDtypeStruct(half, F32), jax.ShapeDtypeStruct(half, BF16)),
        in_specs=[pl.BlockSpec(memory_space=pltpu.SMEM)] + [vmem] * 4 + [hbm] * (3 + len(pieces)),
        out_specs=(vmem, vmem),
        scratch_shapes=[
            pltpu.VMEM((4, 2, 2, 8, 2, 3 * PART, width), BF16),
            pltpu.VMEM((2,) + sides[0].shape, BF16),
            pltpu.VMEM((2 * layers, rows, width), BF16),
            pltpu.VMEM((2 * layers, rows, width), BF16),
            pltpu.VMEM((2 * layers, rows, rank), BF16),
            pltpu.VMEM((2 * layers, rows, width), F32),
            pltpu.VMEM((layers, rows, width), BF16),
            pltpu.VMEM((layers, rows, rank), BF16),
            pltpu.VMEM((2 * layers, rows, 1), F32),
            pltpu.VMEM((rows, width), F32),
            pltpu.SemaphoreType.DMA((SIZES["x"],)),
            pltpu.SemaphoreType.DMA((2,)),
        ],
        compiler_params=pltpu.CompilerParams(vmem_limit_bytes=61 * 1024 * 1024),
        name="row_gradients",
    )(place, latent, target, camera, modulation, *sides, last, *pieces)


def device_number(x, y, z, core):
    return (x * 2 + y // 2) * 32 + (y % 2) * 16 + z * 2 + core


def route(axis, sign):
    pairs = []
    for x in range(SIZES["x"]):
        for y in range(SIZES["y"]):
            for z in range(SIZES["z"]):
                for core in range(2):
                    to = {"x": x, "y": y, "z": z}
                    step = sign if core == 0 else -sign
                    if axis == "half":
                        to["y"] = SIZES["y"] - 1 - y
                    else:
                        to[axis] = (to[axis] + step) % SIZES[axis]
                    pairs.append((device_number(x, y, z, core), device_number(core=core, **to)))
    return pairs


def other_core(block):
    pairs = [(i, i ^ 1) for i in range(256)]
    return lax.ppermute(block, EVERYWHERE, pairs)


def together(*arrays):
    return lax.optimization_barrier(arrays)


def onwards(block, axis):
    return lax.ppermute(block, EVERYWHERE, route(axis, 1))


def back(block, axis):
    return lax.ppermute(block, EVERYWHERE, route(axis, -1))


def ring_blocks(block, axis):
    a = onwards(block, axis)
    return [block, a, back(block, axis), onwards(a, axis)]


def in_line(blocks, place, axis, before=0, split=1):
    count = len(blocks)
    rows = blocks[0].shape[-2] // split
    shape = blocks[0].shape[:-2] + (rows, blocks[0].shape[-1])
    shape = shape[:before] + (count,) + shape[before:]

    def body(place_ref, *refs):
        for i, offset in enumerate(ring_offsets(count)):
            if axis == "half":
                at = lax.rem(place_ref[1] // 2 + offset, 2)
            else:
                sense = 1 - 2 * place_ref[3]
                at = place_ref[list(SIZES).index(axis)] - sense * offset
                at = lax.rem(at + 2 * count, count)
            for half in range(split):
                block = refs[i][..., half * rows : (half + 1) * rows, :]
                out = refs[count + half]
                if before == 0:
                    out[at] = block
                else:
                    out[:, at] = block

    vmem = pl.BlockSpec(memory_space=pltpu.VMEM)
    out_shape = (jax.ShapeDtypeStruct(shape, blocks[0].dtype),) * split
    return pl.pallas_call(
        body,
        out_shape=out_shape,
        in_specs=[pl.BlockSpec(memory_space=pltpu.SMEM)] + [vmem] * count,
        out_specs=(vmem,) * split,
        compiler_params=pltpu.CompilerParams(vmem_limit_bytes=8 * 1024 * 1024),
        name="in_line_" + axis,
    )(place, *blocks)


def gathered_rows(rows, side, place):
    width = rows.shape[1]
    c, ab = rows[2 * PART :], rows[: 2 * PART]
    c1, c2, z1, y1 = onwards(c, "y"), back(c, "y"), onwards(ab, "z"), back(ab, "z")
    c1, c2, z1, y1 = together(c1, c2, z1, y1)
    c3, z2, y2 = together(onwards(c1, "y"), onwards(z1, "z"), back(y1, "z"))
    c = in_line([c, c1, c2, c3], place, "y")[0]
    side, z2 = together(side, z2)
    half = onwards(side, "half")
    c1, c2, z3, y3 = together(onwards(c, "x"), back(c, "x"), onwards(z2, "z"), back(y2, "z"))
    c3, z4, half = together(onwards(c1, "x"), onwards(z3, "z"), half)
    c = in_line([c, c1, c2, c3], place, "x")[0]
    same_line = [[16 * low + i for i in range(16)] for low in range(2)]
    last = lax.all_gather(
        c.reshape(4, 2, 2, PART, width), "dp", axis=0, tiled=False, axis_index_groups=same_line
    )
    a, b = in_line([ab, z1, y1, z2, y2, z3, y3, z4], place, "z", split=2)
    a = in_line(ring_blocks(a, "y"), place, "y")[0].reshape(2, 2, 8, PART, width)
    b = in_line(ring_blocks(b, "x"), place, "x")[0]
    side = in_line(ring_blocks(in_line([side, half], place, "half")[0], "x"), place, "x")[0]
    a1, b1 = onwards(a, "x"), onwards(b, "y")
    a2, b2 = back(a, "x"), back(b, "y")
    small = onwards(a[0, 0, 0], "x")
    a0, b0, side, _ = together(a, b, side, small)
    a3, b3 = onwards(a1, "x"), onwards(b1, "y")
    pieces = []
    for mine in ([a0, a1, a2, a3], [b0, b1, b2, b3]):
        pieces += mine + [other_core(piece) for piece in mine]
    return last, pieces, (side, other_core(side))


def exchange_and_add(parts, axis, groups=None):
    received = lax.all_to_all(parts, axis, 0, 0, axis_index_groups=groups, tiled=True)
    return received.astype(F32).sum(0)


def local(
    latent,
    target,
    camera_of_token,
    timestep_indices,
    camera_embedding_table,
    timestep_embedding_table,
    layer_norm_gain,
    frozen_weight,
    adapter_down_weight,
    adapter_up_weight,
):
    sections = lax.axis_size("section")
    dp_size = lax.axis_size("dp")
    section = lax.axis_index("section")
    lane = lax.axis_index("dp")
    rank, width = adapter_down_weight.shape[1:]
    rows = latent.shape[0] // sections
    scale_factor = 1.0 / math.sqrt(latent.shape[0] * dp_size)
    place = jnp.stack(
        [section // 2, lax.rem(section, 2) * 2 + lane // 16, lax.rem(lane // 2, 8), lax.rem(lane, 2)]
    ).astype(jnp.int32)
    gain = layer_norm_gain
    high = lax.reduce_precision(gain, 8, 7)
    middle = lax.reduce_precision(gain - high, 8, 7)
    lowest = gain - high - middle
    gain_rows = jnp.concatenate([high, middle, lowest, jnp.zeros((EXTRA - 3, width), F32)], axis=0)
    adapter = jnp.where(place[3] == 0, adapter_down_weight[0], adapter_up_weight[0])
    side = jnp.concatenate([adapter, gain_rows.astype(BF16)], axis=0)
    last, pieces, sides = gathered_rows(frozen_weight[0], side, place)

    def my_rows(a):
        return lax.dynamic_slice_in_dim(a, section * rows, rows, 0)

    camera_rows = jnp.dot(
        jax.nn.one_hot(my_rows(camera_of_token), camera_embedding_table.shape[0], dtype=BF16),
        camera_embedding_table,
        preferred_element_type=F32,
    )
    modulation = 1.0 + jnp.dot(
        jax.nn.one_hot(timestep_indices, timestep_embedding_table.shape[0], dtype=BF16),
        timestep_embedding_table,
        preferred_element_type=F32,
    )
    keep, send = row_gradients(
        place,
        my_rows(latent),
        my_rows(target),
        camera_rows,
        modulation,
        sides,
        last,
        pieces,
        sections,
        rank,
        width // dp_size,
        scale_factor,
    )
    on_chip = (keep + other_core(send).astype(F32)).astype(BF16)
    over_sections = exchange_and_add(on_chip, "section")
    same_core = [[i for i in range(32) if i % 2 == core] for core in range(2)]
    summed = exchange_and_add(over_sections.astype(BF16), "dp", same_core)
    turned = summed.T
    return turned[None, :rank], turned[None, rank:]


def solution(mesh):
    in_specs = (
        P("dp", None),
        P("dp", None),
        P("dp"),
        P(),
        P(),
        P(),
        P("section", None),
        P("section", "dp", None),
        P("section", None, None),
        P("section", None, None),
    )
    out_specs = (P("section", None, "dp"), P("section", None, "dp"))
    return jax.shard_map(local, mesh=mesh, in_specs=in_specs, out_specs=out_specs, check_vma=False)
```

```python
import math

import jax
import jax.numpy as jnp
from jax import lax
from jax.experimental import pallas as pl
from jax.experimental.pallas import tpu as pltpu
from jax.sharding import PartitionSpec as P

BLEND = 0.5
ADAPTER_SCALE = 0.5
EPSILON = 1e-06
EXTRA = 8
EVERYWHERE = ("section", "dp")
SIZES = {"x": 4, "y": 4, "z": 8}
PART = 16
F32 = jnp.float32
BF16 = jnp.bfloat16


def dot_nn(a, b):
    return lax.dot_general(a, b, (((1,), (0,)), ((), ())), preferred_element_type=F32)


def dot_nt(a, b):
    return lax.dot_general(a, b, (((1,), (1,)), ((), ())), preferred_element_type=F32)


def dot_tn(a, b):
    return lax.dot_general(a, b, (((0,), (0,)), ((), ())), preferred_element_type=F32)


def ring_offsets(count):
    offsets = [0]
    for distance in range(1, count // 2 + 1):
        offsets.append(distance)
        if 2 * distance < count:
            offsets.append(-distance)
    return offsets


def rows_kernel(
    layers,
    rank,
    scale_factor,
    place_ref,
    latent_ref,
    target_ref,
    camera_ref,
    modulation_ref,
    *refs,
):
    piece_total = 2 * (SIZES["x"] + SIZES["y"])
    sides = refs[:2]
    last = refs[2]
    refs = refs[3:]
    pieces = refs[:piece_total]
    keep_ref, send_ref = refs[piece_total : piece_total + 2]
    run_rows(
        layers,
        rank,
        scale_factor,
        place_ref,
        latent_ref,
        target_ref,
        camera_ref,
        modulation_ref,
        sides,
        last,
        pieces,
        keep_ref,
        send_ref,
        *refs[piece_total + 2 :],
    )


def run_rows(
    layers,
    rank,
    scale_factor,
    place_ref,
    latent_ref,
    target_ref,
    camera_ref,
    modulation_ref,
    sides,
    last,
    pieces,
    keep_ref,
    send_ref,
    weights,
    side,
    hidden_store,
    normed_store,
    low_store,
    slope_store,
    grad_store,
    lowgrad_store,
    inverse_store,
    adjoint,
    sem,
    side_sem,
):
    rows, width = latent_ref.shape
    core = place_ref[3]

    for half in range(2):
        owner = core if half == 0 else 1 - core
        pltpu.make_async_copy(sides[half], side.at[owner], side_sem.at[half]).start()
    count = SIZES["x"]
    arrivals = [
        (half, i, core if half == 0 else 1 - core, offset)
        for half in range(2)
        for i, offset in enumerate(ring_offsets(count))
    ]

    def position(axis, owner, offset):
        return lax.rem(place_ref[axis] - (1 - 2 * owner) * offset + 2 * count, count)

    def fetch(x):
        for half, i, owner, offset in arrivals:
            home = weights.at[x, :, :, :, owner, pl.ds(0, PART)]
            one = pltpu.make_async_copy(pieces[count * half + i], home, sem.at[x])
            pl.when(position(0, owner, offset) == x)(one.start)
            at = position(1, owner, offset)
            home = weights.at[x, at // 2, lax.rem(at, 2), :, owner, pl.ds(PART, PART)]
            block = pieces[count * (2 + half) + i]
            pltpu.make_async_copy(block.at[x], home, sem.at[x]).start()
        for z in range(SIZES["z"]):
            for owner in range(2):
                home = weights.at[x, :, :, z, owner, pl.ds(2 * PART, PART)]
                pltpu.make_async_copy(last.at[2 * z + owner, x], home, sem.at[x]).start()

    fetch(0)

    def arrive(x):
        pltpu.make_async_copy(weights.at[x], weights.at[x], sem.at[x]).wait()

    def weight(layer):
        return weights[layer // 2, lax.rem(layer, 2)].reshape(width, width)

    def adapter(layer):
        x, h = layer // 2, lax.rem(layer, 2)
        return side[0, x, h, 0:rank], side[1, x, h, 0:rank]

    def scale_row(layer, step):
        parts = side[0, layer // 2, lax.rem(layer, 2), rank:].astype(F32)
        gain = (parts[0:1] + parts[1:2]) + parts[2:3]
        return gain * modulation_ref[pl.ds(step, 1), :]

    def forward(step, layer, hidden):
        slot = step * layers + layer
        hidden_store[slot] = hidden
        down, up = adapter(layer)
        hf = hidden.astype(F32)
        inverse = lax.rsqrt(jnp.mean(hf * hf, axis=-1, keepdims=True) + EPSILON)
        inverse_store[slot] = inverse
        normed = (hf * inverse * scale_row(layer, step)).astype(BF16)
        low = dot_nt(normed, down).astype(BF16)
        pre = ADAPTER_SCALE * dot_nn(low, up) + dot_nn(normed, weight(layer))
        normed_store[slot] = normed
        low_store[slot] = low
        s = jax.nn.sigmoid(pre)
        slope_store[slot] = s * (1.0 + pre * (1.0 - s))
        return (hf + pre * s).astype(BF16)

    latent = latent_ref[...].astype(F32)
    camera = camera_ref[...]
    for half in range(2):
        owner = core if half == 0 else 1 - core
        pltpu.make_async_copy(sides[half], side.at[owner], side_sem.at[half]).wait()

    def first_pass(layer, h):
        x = layer // 2
        first = lax.rem(layer, 2) == 0
        pl.when(first)(lambda: arrive(x))
        pl.when(first & (x + 1 < count))(lambda: fetch(x + 1))
        return forward(0, layer, h)

    hidden = lax.fori_loop(0, layers, first_pass, (latent + camera).astype(BF16))
    middle = (BLEND * (latent + hidden.astype(F32))).astype(BF16).astype(F32)
    hidden = lax.fori_loop(
        0, layers, lambda layer, h: forward(1, layer, h), (middle + camera).astype(BF16)
    )
    squashed = jnp.tanh(BLEND * (middle + hidden.astype(F32)))
    adjoint[...] = target_ref[...].astype(F32) * (1.0 - squashed * squashed) * scale_factor

    def backward(step, layer, cotangent):
        slot = step * layers + layer
        down, up = adapter(layer)
        pre_grad = (cotangent * slope_store[slot]).astype(BF16)
        low_grad = (ADAPTER_SCALE * dot_nt(pre_grad, up)).astype(BF16)
        norm_grad = dot_nn(low_grad, down) + dot_nt(pre_grad, weight(layer))
        hf = hidden_store[slot].astype(F32)
        inverse = inverse_store[slot]
        y = hf * inverse
        g = norm_grad * scale_row(layer, step)
        result = cotangent + inverse * (g - y * jnp.mean(g * y, axis=-1, keepdims=True))
        return pre_grad, low_grad, result.astype(BF16).astype(F32)

    def last_step(i, cotangent):
        layer = layers - 1 - i
        pre_grad, low_grad, result = backward(1, layer, cotangent)
        grad_store[layer] = pre_grad
        lowgrad_store[layer] = low_grad
        return result

    def first_step(i, cotangent):
        layer = layers - 1 - i
        pre_grad, low_grad, result = backward(0, layer, cotangent)
        both = layers + layer
        pre_both = jnp.concatenate([pre_grad, grad_store[layer]], axis=0)
        lg_both = jnp.concatenate([low_grad, lowgrad_store[layer]], axis=0)
        low_both = jnp.concatenate([low_store[layer], low_store[both]], axis=0)
        normed_both = jnp.concatenate([normed_store[layer], normed_store[both]], axis=0)
        for first, term in (
            (0, dot_tn(normed_both, lg_both)),
            (rank, ADAPTER_SCALE * dot_tn(pre_both, low_both)),
        ):
            columns = term.reshape(-1, 2, keep_ref.shape[2], rank)
            here = core == 0
            keep_ref[layer, :, :, first : first + rank] = jnp.where(
                here, columns[:, 0], columns[:, 1]
            ).astype(BF16)
            send_ref[layer, :, :, first : first + rank] = jnp.where(
                here, columns[:, 1], columns[:, 0]
            ).astype(BF16)
        return result

    entering = lax.fori_loop(0, layers, last_step, BLEND * adjoint[...])
    lax.fori_loop(0, layers, first_step, BLEND * (BLEND * adjoint[...] + entering))


def row_gradients(
    place, latent, target, camera, modulation, sides, last, pieces, layers, rank, chunk, scale_factor
):
    rows, width = latent.shape
    vmem = pl.BlockSpec(memory_space=pltpu.VMEM)
    hbm = pl.BlockSpec(memory_space=pltpu.HBM)
    half = (layers, width // (2 * chunk), chunk, 2 * rank)

    def body(*refs):
        rows_kernel(layers, rank, scale_factor, *refs)

    return pl.pallas_call(
        body,
        out_shape=(jax.ShapeDtypeStruct(half, BF16), jax.ShapeDtypeStruct(half, BF16)),
        in_specs=[pl.BlockSpec(memory_space=pltpu.SMEM)] + [vmem] * 4 + [hbm] * (3 + len(pieces)),
        out_specs=(vmem, vmem),
        scratch_shapes=[
            pltpu.VMEM((4, 2, 2, 8, 2, 3 * PART, width), BF16),
            pltpu.VMEM((2,) + sides[0].shape, BF16),
            pltpu.VMEM((2 * layers, rows, width), BF16),
            pltpu.VMEM((2 * layers, rows, width), BF16),
            pltpu.VMEM((2 * layers, rows, rank), BF16),
            pltpu.VMEM((2 * layers, rows, width), F32),
            pltpu.VMEM((layers, rows, width), BF16),
            pltpu.VMEM((layers, rows, rank), BF16),
            pltpu.VMEM((2 * layers, rows, 1), F32),
            pltpu.VMEM((rows, width), F32),
            pltpu.SemaphoreType.DMA((SIZES["x"],)),
            pltpu.SemaphoreType.DMA((2,)),
        ],
        compiler_params=pltpu.CompilerParams(vmem_limit_bytes=61 * 1024 * 1024),
        name="row_gradients",
    )(place, latent, target, camera, modulation, *sides, last, *pieces)


def device_number(x, y, z, core):
    return (x * 2 + y // 2) * 32 + (y % 2) * 16 + z * 2 + core


def route(axis, sign):
    pairs = []
    for x in range(SIZES["x"]):
        for y in range(SIZES["y"]):
            for z in range(SIZES["z"]):
                for core in range(2):
                    to = {"x": x, "y": y, "z": z}
                    step = sign if core == 0 else -sign
                    if axis == "half":
                        to["y"] = SIZES["y"] - 1 - y
                    else:
                        to[axis] = (to[axis] + step) % SIZES[axis]
                    pairs.append((device_number(x, y, z, core), device_number(core=core, **to)))
    return pairs


def other_core(block):
    pairs = [(i, i ^ 1) for i in range(256)]
    return lax.ppermute(block, EVERYWHERE, pairs)


def together(*arrays):
    return lax.optimization_barrier(arrays)


def onwards(block, axis):
    return lax.ppermute(block, EVERYWHERE, route(axis, 1))


def back(block, axis):
    return lax.ppermute(block, EVERYWHERE, route(axis, -1))


def ring_blocks(block, axis):
    a = onwards(block, axis)
    return [block, a, back(block, axis), onwards(a, axis)]


def in_line(blocks, place, axis, before=0, split=1):
    count = len(blocks)
    rows = blocks[0].shape[-2] // split
    shape = blocks[0].shape[:-2] + (rows, blocks[0].shape[-1])
    shape = shape[:before] + (count,) + shape[before:]

    def body(place_ref, *refs):
        for i, offset in enumerate(ring_offsets(count)):
            if axis == "half":
                at = lax.rem(place_ref[1] // 2 + offset, 2)
            else:
                sense = 1 - 2 * place_ref[3]
                at = place_ref[list(SIZES).index(axis)] - sense * offset
                at = lax.rem(at + 2 * count, count)
            for half in range(split):
                block = refs[i][..., half * rows : (half + 1) * rows, :]
                out = refs[count + half]
                if before == 0:
                    out[at] = block
                else:
                    out[:, at] = block

    vmem = pl.BlockSpec(memory_space=pltpu.VMEM)
    out_shape = (jax.ShapeDtypeStruct(shape, blocks[0].dtype),) * split
    return pl.pallas_call(
        body,
        out_shape=out_shape,
        in_specs=[pl.BlockSpec(memory_space=pltpu.SMEM)] + [vmem] * count,
        out_specs=(vmem,) * split,
        compiler_params=pltpu.CompilerParams(vmem_limit_bytes=8 * 1024 * 1024),
        name="in_line_" + axis,
    )(place, *blocks)


def gathered_rows(rows, side, place):
    width = rows.shape[1]
    c, ab = rows[2 * PART :], rows[: 2 * PART]
    c1, c2, z1, y1 = onwards(c, "y"), back(c, "y"), onwards(ab, "z"), back(ab, "z")
    c1, c2, z1, y1 = together(c1, c2, z1, y1)
    c3, z2, y2 = together(onwards(c1, "y"), onwards(z1, "z"), back(y1, "z"))
    c = in_line([c, c1, c2, c3], place, "y")[0]
    side, z2 = together(side, z2)
    half = onwards(side, "half")
    c1, c2, z3, y3 = together(onwards(c, "x"), back(c, "x"), onwards(z2, "z"), back(y2, "z"))
    c3, z4, half = together(onwards(c1, "x"), onwards(z3, "z"), half)
    c = in_line([c, c1, c2, c3], place, "x")[0]
    same_line = [[16 * low + i for i in range(16)] for low in range(2)]
    last = lax.all_gather(
        c.reshape(4, 2, 2, PART, width), "dp", axis=0, tiled=False, axis_index_groups=same_line
    )
    a, b = in_line([ab, z1, y1, z2, y2, z3, y3, z4], place, "z", split=2)
    a = in_line(ring_blocks(a, "y"), place, "y")[0].reshape(2, 2, 8, PART, width)
    b = in_line(ring_blocks(b, "x"), place, "x")[0]
    side = in_line(ring_blocks(in_line([side, half], place, "half")[0], "x"), place, "x")[0]
    a1, b1 = onwards(a, "x"), onwards(b, "y")
    a2, b2 = back(a, "x"), back(b, "y")
    a0, b0, side = together(a, b, side)
    a3, b3 = onwards(a1, "x"), onwards(b1, "y")
    pieces = []
    for mine in ([a0, a1, a2, a3], [b0, b1, b2, b3]):
        pieces += mine + [other_core(piece) for piece in mine]
    return last, pieces, (side, other_core(side))


def exchange_and_add(parts, axis, groups=None):
    received = lax.all_to_all(parts, axis, 0, 0, axis_index_groups=groups, tiled=True)
    return received.astype(F32).sum(0)


def local(
    latent,
    target,
    camera_of_token,
    timestep_indices,
    camera_embedding_table,
    timestep_embedding_table,
    layer_norm_gain,
    frozen_weight,
    adapter_down_weight,
    adapter_up_weight,
):
    sections = lax.axis_size("section")
    dp_size = lax.axis_size("dp")
    section = lax.axis_index("section")
    lane = lax.axis_index("dp")
    rank, width = adapter_down_weight.shape[1:]
    rows = latent.shape[0] // sections
    scale_factor = 1.0 / math.sqrt(latent.shape[0] * dp_size)
    place = jnp.stack(
        [section // 2, lax.rem(section, 2) * 2 + lane // 16, lax.rem(lane // 2, 8), lax.rem(lane, 2)]
    ).astype(jnp.int32)
    gain = layer_norm_gain
    high = lax.reduce_precision(gain, 8, 7)
    middle = lax.reduce_precision(gain - high, 8, 7)
    lowest = gain - high - middle
    gain_rows = jnp.concatenate([high, middle, lowest, jnp.zeros((EXTRA - 3, width), F32)], axis=0)
    adapter = jnp.where(place[3] == 0, adapter_down_weight[0], adapter_up_weight[0])
    side = jnp.concatenate([adapter, gain_rows.astype(BF16)], axis=0)
    last, pieces, sides = gathered_rows(frozen_weight[0], side, place)

    def my_rows(a):
        return lax.dynamic_slice_in_dim(a, section * rows, rows, 0)

    camera_rows = jnp.dot(
        jax.nn.one_hot(my_rows(camera_of_token), camera_embedding_table.shape[0], dtype=BF16),
        camera_embedding_table,
        preferred_element_type=F32,
    )
    modulation = 1.0 + jnp.dot(
        jax.nn.one_hot(timestep_indices, timestep_embedding_table.shape[0], dtype=BF16),
        timestep_embedding_table,
        preferred_element_type=F32,
    )
    keep, send = row_gradients(
        place,
        my_rows(latent),
        my_rows(target),
        camera_rows,
        modulation,
        sides,
        last,
        pieces,
        sections,
        rank,
        width // dp_size,
        scale_factor,
    )
    on_chip = (keep.astype(F32) + other_core(send).astype(F32)).astype(BF16)
    over_sections = exchange_and_add(on_chip, "section")
    same_core = [[i for i in range(32) if i % 2 == core] for core in range(2)]
    summed = exchange_and_add(over_sections.astype(BF16), "dp", same_core)
    turned = summed.T
    return turned[None, :rank], turned[None, rank:]


def solution(mesh):
    in_specs = (
        P("dp", None),
        P("dp", None),
        P("dp"),
        P(),
        P(),
        P(),
        P("section", None),
        P("section", "dp", None),
        P("section", None, None),
        P("section", None, None),
    )
    out_specs = (P("section", None, "dp"), P("section", None, "dp"))
    return jax.shard_map(local, mesh=mesh, in_specs=in_specs, out_specs=out_specs, check_vma=False)
```

```python
import math

import jax
import jax.numpy as jnp
from jax import lax
from jax.experimental import pallas as pl
from jax.experimental.pallas import tpu as pltpu
from jax.sharding import PartitionSpec as P

BLEND = 0.5
ADAPTER_SCALE = 0.5
EPSILON = 1e-06
EXTRA = 8
EVERYWHERE = ("section", "dp")
SIZES = {"x": 4, "y": 4, "z": 8}
PART = 16
F32 = jnp.float32
BF16 = jnp.bfloat16


def dot_nn(a, b):
    return lax.dot_general(a, b, (((1,), (0,)), ((), ())), preferred_element_type=F32)


def dot_nt(a, b):
    return lax.dot_general(a, b, (((1,), (1,)), ((), ())), preferred_element_type=F32)


def dot_tn(a, b):
    return lax.dot_general(a, b, (((0,), (0,)), ((), ())), preferred_element_type=F32)


def ring_offsets(count):
    offsets = [0]
    for distance in range(1, count // 2 + 1):
        offsets.append(distance)
        if 2 * distance < count:
            offsets.append(-distance)
    return offsets


def rows_kernel(
    layers,
    rank,
    scale_factor,
    place_ref,
    latent_ref,
    target_ref,
    camera_ref,
    modulation_ref,
    *refs,
):
    piece_total = 2 * (SIZES["x"] + SIZES["y"])
    sides = refs[:2]
    last = refs[2]
    refs = refs[3:]
    pieces = refs[:piece_total]
    keep_ref, send_ref = refs[piece_total : piece_total + 2]
    run_rows(
        layers,
        rank,
        scale_factor,
        place_ref,
        latent_ref,
        target_ref,
        camera_ref,
        modulation_ref,
        sides,
        last,
        pieces,
        keep_ref,
        send_ref,
        *refs[piece_total + 2 :],
    )


def run_rows(
    layers,
    rank,
    scale_factor,
    place_ref,
    latent_ref,
    target_ref,
    camera_ref,
    modulation_ref,
    sides,
    last,
    pieces,
    keep_ref,
    send_ref,
    weights,
    side,
    hidden_store,
    normed_store,
    low_store,
    slope_store,
    grad_store,
    lowgrad_store,
    inverse_store,
    adjoint,
    sem,
    side_sem,
):
    rows, width = latent_ref.shape
    core = place_ref[3]

    for half in range(2):
        owner = core if half == 0 else 1 - core
        pltpu.make_async_copy(sides[half], side.at[owner], side_sem.at[half]).start()
    count = SIZES["x"]
    arrivals = [
        (half, i, core if half == 0 else 1 - core, offset)
        for half in range(2)
        for i, offset in enumerate(ring_offsets(count))
    ]

    def position(axis, owner, offset):
        return lax.rem(place_ref[axis] - (1 - 2 * owner) * offset + 2 * count, count)

    def fetch(x):
        for half, i, owner, offset in arrivals:
            home = weights.at[x, :, :, :, owner, pl.ds(0, PART)]
            one = pltpu.make_async_copy(pieces[count * half + i], home, sem.at[x])
            pl.when(position(0, owner, offset) == x)(one.start)
            at = position(1, owner, offset)
            home = weights.at[x, at // 2, lax.rem(at, 2), :, owner, pl.ds(PART, PART)]
            block = pieces[count * (2 + half) + i]
            pltpu.make_async_copy(block.at[x], home, sem.at[x]).start()
        for z in range(SIZES["z"]):
            for owner in range(2):
                home = weights.at[x, :, :, z, owner, pl.ds(2 * PART, PART)]
                pltpu.make_async_copy(last.at[2 * z + owner, x], home, sem.at[x]).start()

    fetch(0)

    def arrive(x):
        pltpu.make_async_copy(weights.at[x], weights.at[x], sem.at[x]).wait()

    def weight(layer):
        return weights[layer // 2, lax.rem(layer, 2)].reshape(width, width)

    def adapter(layer):
        x, h = layer // 2, lax.rem(layer, 2)
        return side[0, x, h, 0:rank], side[1, x, h, 0:rank]

    def scale_row(layer, step):
        parts = side[0, layer // 2, lax.rem(layer, 2), rank:].astype(F32)
        gain = (parts[0:1] + parts[1:2]) + parts[2:3]
        return gain * modulation_ref[pl.ds(step, 1), :]

    def forward(step, layer, hidden):
        slot = step * layers + layer
        hidden_store[slot] = hidden
        down, up = adapter(layer)
        hf = hidden.astype(F32)
        inverse = lax.rsqrt(jnp.mean(hf * hf, axis=-1, keepdims=True) + EPSILON)
        inverse_store[slot] = inverse
        normed = (hf * inverse * scale_row(layer, step)).astype(BF16)
        low = dot_nt(normed, down).astype(BF16)
        pre = ADAPTER_SCALE * dot_nn(low, up) + dot_nn(normed, weight(layer))
        normed_store[slot] = normed
        low_store[slot] = low
        s = jax.nn.sigmoid(pre)
        slope_store[slot] = s * (1.0 + pre * (1.0 - s))
        return (hf + pre * s).astype(BF16)

    latent = latent_ref[...].astype(F32)
    camera = camera_ref[...]
    for half in range(2):
        owner = core if half == 0 else 1 - core
        pltpu.make_async_copy(sides[half], side.at[owner], side_sem.at[half]).wait()

    def first_pass(layer, h):
        x = layer // 2
        first = lax.rem(layer, 2) == 0
        pl.when(first)(lambda: arrive(x))
        pl.when(first & (x + 1 < count))(lambda: fetch(x + 1))
        return forward(0, layer, h)

    hidden = lax.fori_loop(0, layers, first_pass, (latent + camera).astype(BF16))
    middle = (BLEND * (latent + hidden.astype(F32))).astype(BF16).astype(F32)
    hidden = lax.fori_loop(
        0, layers, lambda layer, h: forward(1, layer, h), (middle + camera).astype(BF16)
    )
    squashed = jnp.tanh(BLEND * (middle + hidden.astype(F32)))
    adjoint[...] = target_ref[...].astype(F32) * (1.0 - squashed * squashed) * scale_factor

    def backward(step, layer, cotangent):
        slot = step * layers + layer
        down, up = adapter(layer)
        pre_grad = (cotangent * slope_store[slot]).astype(BF16)
        low_grad = (ADAPTER_SCALE * dot_nt(pre_grad, up)).astype(BF16)
        norm_grad = dot_nn(low_grad, down) + dot_nt(pre_grad, weight(layer))
        hf = hidden_store[slot].astype(F32)
        inverse = inverse_store[slot]
        y = hf * inverse
        g = norm_grad * scale_row(layer, step)
        result = cotangent + inverse * (g - y * jnp.mean(g * y, axis=-1, keepdims=True))
        return pre_grad, low_grad, result.astype(BF16).astype(F32)

    def last_step(i, cotangent):
        layer = layers - 1 - i
        pre_grad, low_grad, result = backward(1, layer, cotangent)
        grad_store[layer] = pre_grad
        lowgrad_store[layer] = low_grad
        return result

    def first_step(i, cotangent):
        layer = layers - 1 - i
        pre_grad, low_grad, result = backward(0, layer, cotangent)
        both = layers + layer
        pre_both = jnp.concatenate([pre_grad, grad_store[layer]], axis=0)
        lg_both = jnp.concatenate([low_grad, lowgrad_store[layer]], axis=0)
        low_both = jnp.concatenate([low_store[layer], low_store[both]], axis=0)
        normed_both = jnp.concatenate([normed_store[layer], normed_store[both]], axis=0)
        for first, term in (
            (0, dot_tn(normed_both, lg_both)),
            (rank, ADAPTER_SCALE * dot_tn(pre_both, low_both)),
        ):
            columns = term.reshape(-1, 2, keep_ref.shape[2], rank)
            here = core == 0
            keep_ref[layer, :, :, first : first + rank] = jnp.where(
                here, columns[:, 0], columns[:, 1]
            ).astype(BF16)
            send_ref[layer, :, :, first : first + rank] = jnp.where(
                here, columns[:, 1], columns[:, 0]
            ).astype(BF16)
        return result

    entering = lax.fori_loop(0, layers, last_step, BLEND * adjoint[...])
    lax.fori_loop(0, layers, first_step, BLEND * (BLEND * adjoint[...] + entering))


def row_gradients(
    place, latent, target, camera, modulation, sides, last, pieces, layers, rank, chunk, scale_factor
):
    rows, width = latent.shape
    vmem = pl.BlockSpec(memory_space=pltpu.VMEM)
    hbm = pl.BlockSpec(memory_space=pltpu.HBM)
    half = (layers, width // (2 * chunk), chunk, 2 * rank)

    def body(*refs):
        rows_kernel(layers, rank, scale_factor, *refs)

    return pl.pallas_call(
        body,
        out_shape=(jax.ShapeDtypeStruct(half, BF16), jax.ShapeDtypeStruct(half, BF16)),
        in_specs=[pl.BlockSpec(memory_space=pltpu.SMEM)] + [vmem] * 4 + [hbm] * (3 + len(pieces)),
        out_specs=(vmem, vmem),
        scratch_shapes=[
            pltpu.VMEM((4, 2, 2, 8, 2, 3 * PART, width), BF16),
            pltpu.VMEM((2,) + sides[0].shape, BF16),
            pltpu.VMEM((2 * layers, rows, width), BF16),
            pltpu.VMEM((2 * layers, rows, width), BF16),
            pltpu.VMEM((2 * layers, rows, rank), BF16),
            pltpu.VMEM((2 * layers, rows, width), F32),
            pltpu.VMEM((layers, rows, width), BF16),
            pltpu.VMEM((layers, rows, rank), BF16),
            pltpu.VMEM((2 * layers, rows, 1), F32),
            pltpu.VMEM((rows, width), F32),
            pltpu.SemaphoreType.DMA((SIZES["x"],)),
            pltpu.SemaphoreType.DMA((2,)),
        ],
        compiler_params=pltpu.CompilerParams(vmem_limit_bytes=61 * 1024 * 1024),
        name="row_gradients",
    )(place, latent, target, camera, modulation, *sides, last, *pieces)


def device_number(x, y, z, core):
    return (x * 2 + y // 2) * 32 + (y % 2) * 16 + z * 2 + core


def route(axis, sign):
    pairs = []
    for x in range(SIZES["x"]):
        for y in range(SIZES["y"]):
            for z in range(SIZES["z"]):
                for core in range(2):
                    to = {"x": x, "y": y, "z": z}
                    step = sign if core == 0 else -sign
                    if axis == "half":
                        to["y"] = SIZES["y"] - 1 - y
                    else:
                        to[axis] = (to[axis] + step) % SIZES[axis]
                    pairs.append((device_number(x, y, z, core), device_number(core=core, **to)))
    return pairs


def other_core(block):
    pairs = [(i, i ^ 1) for i in range(256)]
    return lax.ppermute(block, EVERYWHERE, pairs)


def together(*arrays):
    return lax.optimization_barrier(arrays)


def onwards(block, axis):
    return lax.ppermute(block, EVERYWHERE, route(axis, 1))


def back(block, axis):
    return lax.ppermute(block, EVERYWHERE, route(axis, -1))


def ring_blocks(block, axis):
    a = onwards(block, axis)
    return [block, a, back(block, axis), onwards(a, axis)]


def in_line(blocks, place, axis, before=0, split=1):
    count = len(blocks)
    rows = blocks[0].shape[-2] // split
    shape = blocks[0].shape[:-2] + (rows, blocks[0].shape[-1])
    shape = shape[:before] + (count,) + shape[before:]

    def body(place_ref, *refs):
        for i, offset in enumerate(ring_offsets(count)):
            if axis == "half":
                at = lax.rem(place_ref[1] // 2 + offset, 2)
            else:
                sense = 1 - 2 * place_ref[3]
                at = place_ref[list(SIZES).index(axis)] - sense * offset
                at = lax.rem(at + 2 * count, count)
            for half in range(split):
                block = refs[i][..., half * rows : (half + 1) * rows, :]
                out = refs[count + half]
                if before == 0:
                    out[at] = block
                else:
                    out[:, at] = block

    vmem = pl.BlockSpec(memory_space=pltpu.VMEM)
    out_shape = (jax.ShapeDtypeStruct(shape, blocks[0].dtype),) * split
    return pl.pallas_call(
        body,
        out_shape=out_shape,
        in_specs=[pl.BlockSpec(memory_space=pltpu.SMEM)] + [vmem] * count,
        out_specs=(vmem,) * split,
        compiler_params=pltpu.CompilerParams(vmem_limit_bytes=8 * 1024 * 1024),
        name="in_line_" + axis,
    )(place, *blocks)


def gathered_rows(rows, side, place):
    width = rows.shape[1]
    c, ab = rows[2 * PART :], rows[: 2 * PART]
    c1, c2, z1, y1 = onwards(c, "y"), back(c, "y"), onwards(ab, "z"), back(ab, "z")
    c1, c2, z1, y1 = together(c1, c2, z1, y1)
    c3, z2, y2 = together(onwards(c1, "y"), onwards(z1, "z"), back(y1, "z"))
    c = in_line([c, c1, c2, c3], place, "y")[0]
    side, z2 = together(side, z2)
    half = onwards(side, "half")
    c1, c2, z3, y3 = together(onwards(c, "x"), back(c, "x"), onwards(z2, "z"), back(y2, "z"))
    c3, z4, half = together(onwards(c1, "x"), onwards(z3, "z"), half)
    c = in_line([c, c1, c2, c3], place, "x")[0]
    same_line = [[16 * low + i for i in range(16)] for low in range(2)]
    last = lax.all_gather(
        c.reshape(4, 2, 2, PART, width), "dp", axis=0, tiled=False, axis_index_groups=same_line
    )
    a, b = in_line([ab, z1, y1, z2, y2, z3, y3, z4], place, "z", split=2)
    a = in_line(ring_blocks(a, "y"), place, "y")[0].reshape(2, 2, 8, PART, width)
    b = in_line(ring_blocks(b, "x"), place, "x")[0]
    side = in_line(ring_blocks(in_line([side, half], place, "half")[0], "x"), place, "x")[0]
    a1, b1 = onwards(a, "x"), onwards(b, "y")
    a2, b2 = back(a, "x"), back(b, "y")
    a3, b3 = onwards(a1, "x"), onwards(b1, "y")
    pieces = []
    for mine in ([a, a1, a2, a3], [b, b1, b2, b3]):
        pieces += mine + [other_core(piece) for piece in mine]
    return last, pieces, (side, other_core(side))


def exchange_and_add(parts, axis, groups=None):
    received = lax.all_to_all(parts, axis, 0, 0, axis_index_groups=groups, tiled=True)
    return received.astype(F32).sum(0)


def local(
    latent,
    target,
    camera_of_token,
    timestep_indices,
    camera_embedding_table,
    timestep_embedding_table,
    layer_norm_gain,
    frozen_weight,
    adapter_down_weight,
    adapter_up_weight,
):
    sections = lax.axis_size("section")
    dp_size = lax.axis_size("dp")
    section = lax.axis_index("section")
    lane = lax.axis_index("dp")
    rank, width = adapter_down_weight.shape[1:]
    rows = latent.shape[0] // sections
    scale_factor = 1.0 / math.sqrt(latent.shape[0] * dp_size)
    place = jnp.stack(
        [section // 2, lax.rem(section, 2) * 2 + lane // 16, lax.rem(lane // 2, 8), lax.rem(lane, 2)]
    ).astype(jnp.int32)
    gain = layer_norm_gain
    high = lax.reduce_precision(gain, 8, 7)
    middle = lax.reduce_precision(gain - high, 8, 7)
    lowest = gain - high - middle
    gain_rows = jnp.concatenate([high, middle, lowest, jnp.zeros((EXTRA - 3, width), F32)], axis=0)
    adapter = jnp.where(place[3] == 0, adapter_down_weight[0], adapter_up_weight[0])
    side = jnp.concatenate([adapter, gain_rows.astype(BF16)], axis=0)
    last, pieces, sides = gathered_rows(frozen_weight[0], side, place)

    def my_rows(a):
        return lax.dynamic_slice_in_dim(a, section * rows, rows, 0)

    camera_rows = jnp.dot(
        jax.nn.one_hot(my_rows(camera_of_token), camera_embedding_table.shape[0], dtype=BF16),
        camera_embedding_table,
        preferred_element_type=F32,
    )
    modulation = 1.0 + jnp.dot(
        jax.nn.one_hot(timestep_indices, timestep_embedding_table.shape[0], dtype=BF16),
        timestep_embedding_table,
        preferred_element_type=F32,
    )
    keep, send = row_gradients(
        place,
        my_rows(latent),
        my_rows(target),
        camera_rows,
        modulation,
        sides,
        last,
        pieces,
        sections,
        rank,
        width // dp_size,
        scale_factor,
    )
    on_chip = (keep.astype(F32) + other_core(send).astype(F32)).astype(BF16)
    over_sections = exchange_and_add(on_chip, "section")
    same_core = [[i for i in range(32) if i % 2 == core] for core in range(2)]
    summed = exchange_and_add(over_sections.astype(BF16), "dp", same_core)
    turned = summed.T
    return turned[None, :rank], turned[None, rank:]


def solution(mesh):
    in_specs = (
        P("dp", None),
        P("dp", None),
        P("dp"),
        P(),
        P(),
        P(),
        P("section", None),
        P("section", "dp", None),
        P("section", None, None),
        P("section", None, None),
    )
    out_specs = (P("section", None, "dp"), P("section", None, "dp"))
    return jax.shard_map(local, mesh=mesh, in_specs=in_specs, out_specs=out_specs, check_vma=False)
```
